32 devices in a mesh: own: 8 (over z, core), help: 4 (over y, x).
Axes of the slice: x: 2, y: 2, z: 4, core: 2. Of those that a mesh axis runs over, the one named last changes fastest.
Arguments:
- records: bfloat16 [16384, 256], P(('own', 'help')), may hold values from -6 to 6
- owner: int32 [16384, 1], P(('own', 'help')), may hold values from 0 to 7; in each aligned block of 512 rows (0 to 511, 512 to 1023, ...) at most 128 rows name the same one
- subkey: int32 [16384], P(('own', 'help')), may hold values from 0 to 3
- source: int32 [16384], P(('own', 'help')), may hold values from 0 to 3
Outputs:
- resolved: bfloat16 [16384, 256], P(('own', 'help'))
The draws below stay inside these ranges and needn't reach their ends.
Inputs may be any that keep to these rules, and one draw needn't show every extreme that they name: Among the 512 records of one device (aligned blocks of rows), no owner is named more than 128 times, and in every draw some device names some owner exactly 128 times.
All inputs are finite; a program needn't handle non-finite values.
Results may differ from the reference program's by a relative error of at most 0.0052.
Values may be sent and summed in bfloat16 or wider, within the bound.
No kernel may reach another device: no remote copies, remote signals or barrier semaphores. Data moves between devices by JAX's collectives and lax.ppermute only.
A program may use at most 192 MiB of HBM per device.

```python
import math
import jax
import jax.numpy as jnp
import numpy as np
from jax import lax

D = 256
R_DEV = 512
SUBKEYS = 4
SOURCES = 4
CAP = 128
SLOTS = 1024
RECORDS = 16384
N_OWN = 8
N_HELP = 4


def touch_ends(drawn, key, low, high):
    index_at = [jax.random.randint(jax.random.fold_in(key, axis), (), 0, length) for axis, length in enumerate(drawn.shape)]
    widest = drawn.shape.index(max(drawn.shape))
    next_to = index_at[:widest] + [(index_at[widest] + 1) % drawn.shape[widest]] + index_at[widest + 1:]
    return drawn.at[tuple(index_at)].set(low).at[tuple(next_to)].set(high)


def steps_of(key, extent, split, least, top_value):
    factor_of = 1.0
    for position, shards_of in split:
        draws = jax.random.uniform(jax.random.fold_in(jax.random.fold_in(key, 6), position), (shards_of,), jnp.float32, least / len(split), top_value / len(split))
        factor_of = factor_of * jnp.repeat(jnp.exp(draws), extent[position] // shards_of).reshape((-1,) + (1,) * (len(extent) - 1 - position))
    return factor_of


def rank_table(number_of, skew):
    portions = [(1 << 20) // math.isqrt(standing ** skew) + 1 for standing in range(1, number_of + 1)]
    scale = 1 + sum(portions) // (1 << 30)
    return np.cumsum(np.array([max(1, weight // scale) for weight in portions]))


def skewed_ids(stream_key, dims, number_of, slope):
    grid = rank_table(number_of, slope)
    ticket = jax.random.randint(jax.random.fold_in(stream_key, 1), dims, 0, int(grid[number_of - 1]))
    standing = jnp.searchsorted(jnp.asarray(grid, jnp.int32), ticket, side="right")
    return jax.random.permutation(jax.random.fold_in(stream_key, 2), number_of)[standing].astype(jnp.int32)


def deal_out(own_key, own, number, rows, amount, top, most, skew):
    sequence = jax.random.permutation(own_key, amount)
    crowded, common = load_shares(amount, rows * top, most, skew, True), load_shares(amount, rows * top, most, skew, False)
    places = jnp.arange(amount)

    def named(lengths, rotation):
        used = int((lengths > 0).sum())
        fixed = max(1, used // 4)
        passed = fixed + (places - fixed + rotation * (used - fixed)) % max(1, amount - fixed)
        return jnp.zeros((amount,), jnp.int32).at[sequence[jnp.where(places < fixed, places, passed)]].set(jnp.asarray(lengths, jnp.int32))

    lengths = jnp.where(number % 4 == 0, named(crowded, number // 4), named(common, number - number // 4 - 1))
    mixed = jax.random.permutation(jax.random.fold_in(own, 3), amount)
    giver, taker = mixed[0:amount // 2 * 2:2], mixed[1:amount // 2 * 2:2]
    room = jnp.minimum(lengths[giver] - 1, most - lengths[taker]) // 2
    room = jnp.where((giver == sequence[0]) | (taker == sequence[0]) | (lengths[taker] == 0), 0, jnp.maximum(room, 0))
    passed = jax.random.randint(jax.random.fold_in(own, 4), (amount // 2,), 0, 1 << 20) % (room + 1)
    lengths = lengths.at[giver].add(-passed).at[taker].add(passed)
    labels = jnp.searchsorted(jnp.cumsum(lengths), jnp.arange(rows * top), side="right").astype(jnp.int32)
    table = labels.reshape(top, rows).T
    table = table[jax.random.permutation(jax.random.fold_in(own, 1), rows)]
    rotation = jax.random.randint(jax.random.fold_in(own, 2), (rows, 1), 0, top)
    return jnp.take_along_axis(table, (jnp.arange(top)[None, :] + rotation) % top, axis=1)


def load_shares(number_of, total, limit, lean, full):
    weights = [(1 << 20) // math.isqrt(grade ** lean) + 1 for grade in range(1, number_of + 1)]
    largest = limit if full else min(limit, max(-(-total // number_of), total * weights[0] // sum(weights)))
    least = 1 if total - largest >= number_of - 1 else 0
    given, surplus = [largest] + [least] * (number_of - 1), total - largest - least * (number_of - 1)
    while surplus > 0:
        movable = [i for i in range(1, number_of) if given[i] < largest] or [i for i in range(1, number_of) if given[i] < limit]
        whole, left = sum([weights[i] for i in movable]), surplus
        for i in movable:
            extra = min(limit - given[i], max(1, left * weights[i] // whole), surplus)
            given[i] = given[i] + extra
            surplus = surplus - extra
    return np.array(given)


def bell_draw(key, extent, scale, reach, shards=(), kind=jnp.bfloat16):
    loudness = steps_of(key, extent, shards, -0.22, 0.18) if shards else 1.0
    drawn = jax.random.normal(key, extent, jnp.float32) * scale * loudness
    return jnp.minimum(jnp.maximum(drawn, -reach), reach).astype(kind)


def setup_inputs(seed: int = 0) -> dict:
    arg_keys = jax.random.split(jax.random.key(seed), 5)
    records = bell_draw(arg_keys[0], (RECORDS, D), 1.0, 6.0, ((0, 32),))
    owner_keys = jax.random.split(jax.random.fold_in(arg_keys[1], 1), RECORDS // R_DEV)
    owner_turns = jax.random.permutation(jax.random.fold_in(arg_keys[1], 3), RECORDS // R_DEV)
    owner = jax.vmap(lambda own, number: deal_out(jax.random.fold_in(arg_keys[1], 2), own, number, R_DEV, N_OWN, 1, CAP, 2))(owner_keys, owner_turns).reshape((RECORDS, 1))
    subkey = touch_ends(skewed_ids(arg_keys[2], (RECORDS,), SUBKEYS, 4), jax.random.fold_in(arg_keys[2], 3), 0, SUBKEYS - 1).astype(jnp.int32)
    source = touch_ends(jax.random.randint(arg_keys[3], (RECORDS,), 0, SOURCES), jax.random.fold_in(arg_keys[3], 1), 0, SOURCES - 1).astype(jnp.int32)
    return dict(records=records, owner=owner, subkey=subkey, source=source)


epsilon = 1e-06
sharpness = 4.0

def normalized(records):
    values_f = records.astype(jnp.float32)
    inverse = lax.rsqrt(lax.optimization_barrier(jnp.mean(values_f * values_f, axis=1, keepdims=True)) + epsilon)
    return (values_f * inverse).astype(jnp.bfloat16)

def pair_weights(query_rows, query_codes, key_rows, key_codes):
    scores = jnp.dot(query_rows, key_rows.T, preferred_element_type=jnp.float32)
    matched = (query_codes[:, None] >= 0) & (key_codes[None, :] >= 0)
    matched = matched & (query_codes[:, None] // SOURCES == key_codes[None, :] // SOURCES)
    matched = matched & (query_codes[:, None] % SOURCES != key_codes[None, :] % SOURCES)
    return jnp.where(matched, jnp.exp(scores * (sharpness / query_rows.shape[1])), jnp.zeros_like(scores))

def resolve(held_rows, partner, mass):
    merged = held_rows.astype(jnp.float32) + partner * lax.rsqrt(1.0 + mass)[:, None]
    return merged.astype(jnp.bfloat16)

def reference(records, owner, subkey, source):
    record_count = records.shape[0]
    device_count = record_count // R_DEV
    scaled = normalized(records)
    target = owner[:, 0]
    onehot = (target.reshape(device_count, R_DEV)[:, :, None] == jnp.arange(N_OWN, dtype=jnp.int32)[None, None, :]).astype(jnp.int32)
    slot_rank = (lax.optimization_barrier(jnp.sum(jnp.cumsum(onehot, axis=1) * onehot, axis=2)) - 1).reshape(record_count)
    device = jnp.arange(record_count, dtype=jnp.int32) // R_DEV
    group_rows = N_HELP * SLOTS
    group_slot = target * group_rows + device % N_HELP * SLOTS + device // N_HELP * CAP + slot_rank
    slot_rows = jnp.zeros((N_OWN * group_rows, D), jnp.bfloat16).at[group_slot].set(scaled)
    slot_codes = jnp.full((N_OWN * group_rows,), -1, jnp.int32).at[group_slot].set(subkey * SOURCES + source)

    def per_owner(owner_index):
        key_rows = lax.dynamic_slice_in_dim(slot_rows, owner_index * group_rows, group_rows, 0)
        key_codes = lax.dynamic_slice_in_dim(slot_codes, owner_index * group_rows, group_rows, 0)

        def per_block(block_index):
            query_rows = lax.dynamic_slice_in_dim(key_rows, block_index * SLOTS, SLOTS, 0)
            query_codes = lax.dynamic_slice_in_dim(key_codes, block_index * SLOTS, SLOTS, 0)
            weight = pair_weights(query_rows, query_codes, key_rows, key_codes)
            partner = jnp.dot(weight.astype(jnp.bfloat16), key_rows, preferred_element_type=jnp.float32)
            mass = lax.optimization_barrier(jnp.sum(weight, axis=1))
            return resolve(query_rows, partner, mass)
        return lax.map(per_block, jnp.arange(N_HELP, dtype=jnp.int32)).reshape(group_rows, D)
    merged = lax.map(per_owner, jnp.arange(N_OWN, dtype=jnp.int32)).reshape(N_OWN * group_rows, D)
    return merged[group_slot]
```

```python
import functools

import jax
import jax.numpy as jnp
from jax import lax
from jax.experimental import pallas as pl
from jax.experimental.pallas import tpu as pltpu
from jax.sharding import Mesh, PartitionSpec as P

SUBKEYS = 4
SOURCES = 4
CODES = SUBKEYS * SOURCES
EPSILON = 1e-06
SHARPNESS = 4.0
LOG2E = 1.4426950408889634
PAD = 8
SWAP = [(0, 1), (1, 0)]
NT = (((1,), (1,)), ((), ()))
VMEM_LIMIT = 48 * 2**20


def selections(full_codes, owner_of, count, cap):
    rows = full_codes.shape[1]
    lines = max(8, count)
    line = lax.broadcasted_iota(jnp.int32, (lines, rows), 0)
    wanted = jnp.full((lines, rows), -1, jnp.int32)
    for j in range(count):
        wanted = jnp.where(line == j, owner_of(j), wanted)
    named = wanted == jnp.broadcast_to(full_codes // CODES, (lines, rows))
    before = lax.broadcasted_iota(jnp.int32, (rows, rows), 0)
    after = lax.broadcasted_iota(jnp.int32, (rows, rows), 1)
    earlier = jnp.where(before < after, 1.0, 0.0).astype(jnp.bfloat16)
    rank = jnp.dot(
        jnp.where(named, 1.0, 0.0).astype(jnp.bfloat16),
        earlier,
        preferred_element_type=jnp.float32,
    )
    rank = jnp.where(named, rank, -1.0).astype(jnp.int32)
    slot = lax.broadcasted_iota(jnp.int32, (cap, rows), 0)
    return [
        jnp.where(slot == rank[j : j + 1, :], 1.0, 0.0).astype(jnp.bfloat16)
        for j in range(count)
    ]


def scale_kernel(rows_ref, owner_ref, subkey_ref, source_ref, out_ref):
    rows, width = rows_ref.shape
    values = rows_ref[...].astype(jnp.float32)
    inverse = lax.rsqrt(jnp.mean(values * values, axis=1, keepdims=True) + EPSILON)
    out_ref[:rows, :] = (values * inverse).astype(jnp.bfloat16)
    codes = (owner_ref[...] * SUBKEYS + subkey_ref[...]) * SOURCES + source_ref[...]
    line = lax.broadcasted_iota(jnp.int32, (PAD, width), 0)
    lines = jnp.zeros((PAD, width), jnp.int32)
    for k in range(rows // width):
        lines = jnp.where(line == k, codes[:, k * width : (k + 1) * width], lines)
    out_ref[rows:, :] = lines.astype(jnp.float32).astype(jnp.bfloat16)


def scale(records, owner, subkey, source):
    rows, width = records.shape
    return pl.pallas_call(
        scale_kernel,
        out_shape=jax.ShapeDtypeStruct((rows + PAD, width), jnp.bfloat16),
        compiler_params=pltpu.CompilerParams(vmem_limit_bytes=VMEM_LIMIT),
    )(records, owner.reshape(1, rows), subkey.reshape(1, rows), source.reshape(1, rows))


def pack_kernel(count, cap, owners_ref, *refs):
    blocks, messages = refs[:2], refs[2:]
    for part in range(2):
        width = blocks[part].shape[1]
        rows = blocks[part].shape[0] - PAD
        scaled = blocks[part][:rows, :]
        lines = blocks[part][rows:, :].astype(jnp.float32)
        full_codes = jnp.concatenate(
            [lines[k : k + 1, :] for k in range(rows // width)], axis=1
        ).astype(jnp.int32)
        codes = jnp.broadcast_to(full_codes % CODES + 1, (8, rows))
        codes = codes.astype(jnp.float32).astype(jnp.bfloat16)
        picks = selections(full_codes, lambda j: owners_ref[0, j], count, cap)
        for j in range(count):
            picked = jnp.dot(picks[j], scaled, preferred_element_type=jnp.float32)
            messages[j][part, :cap, :] = picked.astype(jnp.bfloat16)
            line = lax.dot_general(codes, picks[j], NT, preferred_element_type=jnp.float32)
            messages[j][part, cap:, :] = jnp.zeros((PAD, width), jnp.bfloat16)
            messages[j][part, cap:, :cap] = line.astype(jnp.bfloat16)


def pack(owners, blocks, count, cap):
    shape = jax.ShapeDtypeStruct((2, cap + PAD, blocks[0].shape[1]), jnp.bfloat16)
    return pl.pallas_call(
        functools.partial(pack_kernel, count, cap),
        in_specs=[pl.BlockSpec(memory_space=pltpu.SMEM)]
        + [pl.BlockSpec(memory_space=pltpu.VMEM)] * 2,
        out_specs=[pl.BlockSpec(memory_space=pltpu.VMEM)] * count,
        out_shape=[shape] * count,
        compiler_params=pltpu.CompilerParams(vmem_limit_bytes=VMEM_LIMIT),
    )(owners, *blocks)


def place_kernel(count, cap, owners_ref, owner_ref, out_ref):
    rows = owner_ref.shape[0]
    owner = owner_ref[...]
    lane = lax.broadcasted_iota(jnp.int32, (rows, 128), 1)
    named = owner == lane
    later = lax.broadcasted_iota(jnp.int32, (rows, rows), 0)
    before = lax.broadcasted_iota(jnp.int32, (rows, rows), 1)
    earlier = jnp.where(before < later, 1.0, 0.0).astype(jnp.bfloat16)
    rank = jnp.dot(
        earlier,
        jnp.where(named, 1.0, 0.0).astype(jnp.bfloat16),
        preferred_element_type=jnp.float32,
    )
    rank = jnp.sum(jnp.where(named, rank, 0.0), axis=1, keepdims=True).astype(jnp.int32)
    for i in range(2 * count):
        rank = rank + jnp.where(owner == owners_ref[i // count, i % count], i * cap, 0)
    out_ref[...] = rank


def place(owners, owner, count, cap):
    return pl.pallas_call(
        functools.partial(place_kernel, count, cap),
        in_specs=[
            pl.BlockSpec(memory_space=pltpu.SMEM),
            pl.BlockSpec(memory_space=pltpu.VMEM),
        ],
        out_specs=pl.BlockSpec(memory_space=pltpu.VMEM),
        out_shape=jax.ShapeDtypeStruct(owner.shape, jnp.int32),
        compiler_params=pltpu.CompilerParams(vmem_limit_bytes=VMEM_LIMIT),
    )(owners, owner)


def code_line(ref, part, cap):
    return ref[part, cap : cap + 8, :cap].astype(jnp.float32)[0:1, :].astype(jnp.int32) - 1


def match_kernel(queries, cap, last, *refs):
    outs = refs[-queries:] if last else refs[-2:]
    refs = refs[: -queries] if last else refs[:-2]
    held, refs = refs[:queries], refs[queries:]
    sums, keys = (refs[:2], refs[2:]) if last else (None, refs)
    width = held[0].shape[2]
    diagonal = lax.broadcasted_iota(jnp.int32, (cap, cap), 0) == lax.broadcasted_iota(
        jnp.int32, (cap, cap), 1
    )
    for j in range(queries):
        query = held[j][:, :cap, :].reshape(2 * cap, width)
        span = slice(j * 2 * cap, (j + 1) * 2 * cap)
        columns = []
        for part in range(2):
            line = jnp.broadcast_to(code_line(held[j], part, cap), (cap, cap))
            picked = jnp.where(diagonal, line, 0).astype(jnp.float32)
            columns.append(jnp.sum(picked, axis=1, keepdims=True))
        query_codes = jnp.concatenate(columns, axis=0).astype(jnp.int32)

        def add(key_ref, first, carry):
            total, mass = carry
            pair = key_ref.at[pl.ds(first, 2)]
            key = pair[:, :cap, :].reshape(2 * cap, width)
            key_codes = jnp.concatenate([code_line(pair, k, cap) for k in range(2)], axis=1)
            score = lax.dot_general(query, key, NT, preferred_element_type=jnp.float32)
            differ = query_codes ^ key_codes
            matched = (differ >= 1) & (differ < SOURCES)
            weight = jnp.where(matched, jnp.exp2(score * (SHARPNESS / width * LOG2E)), 0.0)
            mass = mass + jnp.sum(weight, axis=1, keepdims=True)
            return total + jnp.dot(
                weight.astype(jnp.bfloat16), key, preferred_element_type=jnp.float32
            ), mass

        if last:
            carry = sums[0][span, :], sums[1][span, :]
        else:
            carry = jnp.zeros((2 * cap, width), jnp.float32), jnp.zeros((2 * cap, 1), jnp.float32)
        for key_ref in keys:
            pairs = key_ref.shape[0] // 2
            if pairs == 1:
                carry = add(key_ref, 0, carry)
            else:
                carry = lax.fori_loop(
                    0, pairs, lambda i, c, key_ref=key_ref: add(key_ref, 2 * i, c), carry
                )
        total, mass = carry
        if last:
            merged = query.astype(jnp.float32) + total * lax.rsqrt(1.0 + mass)
            outs[j][...] = merged.astype(jnp.bfloat16).reshape(2, cap, width)
        else:
            outs[0][span, :] = total
            outs[1][span, :] = mass


def match(held, keys, cap, sums=None):
    count, width = len(held), held[0].shape[2]
    if sums is None:
        shapes = [
            jax.ShapeDtypeStruct((count * 2 * cap, width), jnp.float32),
            jax.ShapeDtypeStruct((count * 2 * cap, 1), jnp.float32),
        ]
    else:
        shapes = [jax.ShapeDtypeStruct((2, cap, width), jnp.bfloat16)] * count
    operands = (*held, *(sums or ()), *keys)
    return pl.pallas_call(
        functools.partial(match_kernel, count, cap, sums is not None),
        in_specs=[pl.BlockSpec(memory_space=pltpu.VMEM)] * len(operands),
        out_specs=[pl.BlockSpec(memory_space=pltpu.VMEM)] * len(shapes),
        out_shape=shapes,
        compiler_params=pltpu.CompilerParams(vmem_limit_bytes=VMEM_LIMIT),
    )(*operands)


def unpack_kernel(count, cap, place_ref, *refs):
    mine, sibling, out_ref = refs[:count], refs[count : 2 * count], refs[-1]
    rows = out_ref.shape[0]
    slot = lax.broadcasted_iota(jnp.int32, (rows, 2 * count * cap), 1)
    picks = jnp.where(slot == place_ref[...], 1.0, 0.0).astype(jnp.bfloat16)
    blocks = [m[0] for m in mine] + [m[1] for m in sibling]
    out_ref[...] = jnp.dot(
        picks, jnp.concatenate(blocks, axis=0), preferred_element_type=jnp.float32
    ).astype(jnp.bfloat16)


def unpack(places, mine, sibling, cap):
    count, width = len(mine), mine[0].shape[2]
    return pl.pallas_call(
        functools.partial(unpack_kernel, count, cap),
        in_specs=[pl.BlockSpec(memory_space=pltpu.VMEM)] * (2 * count + 1),
        out_specs=pl.BlockSpec(memory_space=pltpu.VMEM),
        out_shape=jax.ShapeDtypeStruct((places.shape[0], width), jnp.bfloat16),
        compiler_params=pltpu.CompilerParams(vmem_limit_bytes=VMEM_LIMIT),
    )(places, *mine, *sibling)


def shards(records, owner, subkey, source):
    row_count = records.shape[0]
    chips = lax.axis_size("z_lo") * lax.axis_size("near")
    near, rest = lax.axis_size("near"), lax.axis_size("far")
    cap = 2 * row_count // chips
    count = chips // 2
    by_hops = sorted(range(chips), key=lambda d: -d.bit_count())
    flips = [[d for d in by_hops if d.bit_count() % 2 == odd] for odd in (1, 0)]
    core = lax.axis_index("core")
    spot = lax.axis_index(("z_lo", "near"))
    table = jnp.array(flips, jnp.int32)
    owners = spot ^ jnp.where(core == 0, table, table[::-1])

    def to_core(x):
        return lax.ppermute(x, "core", SWAP)

    def to_half(x):
        return lax.ppermute(x, "z_hi", SWAP)

    def to_chip(x, j):
        def number(c, s):
            return (s // near * 2 + c) * near + s % near

        pairs = [
            (number(c, s), number(c, s ^ flips[c][j])) for c in range(2) for s in range(chips)
        ]
        return lax.ppermute(x, ("z_lo", "core", "near"), pairs)

    def spread(blocks):
        messages = [to_chip(m, j) for j, m in enumerate(pack(owners, blocks, count, cap))]
        keys = messages
        if rest > 1:
            keys = [lax.all_gather(m, "far", axis=0, tiled=True) for m in messages]
        return messages, keys + [to_core(m) for m in keys]

    block = scale(records, owner, subkey, source)
    far_block = to_half(block)
    held, keys = spread((block, to_core(block)))
    sums = match(held, keys, cap)
    _, far_keys = spread((far_block, to_core(far_block)))
    merged = match(held, far_keys, cap, sums)
    returned = [to_chip(m, j) for j, m in enumerate(merged)]
    places = place(owners, owner, count, cap)
    return unpack(places, returned, [to_core(m) for m in returned], cap)


def solution(mesh):
    own, help_ = mesh.shape["own"], mesh.shape["help"]
    near = 4
    split = Mesh(
        mesh.devices.reshape(2, own // 4, 2, near, help_ // near),
        ("z_hi", "z_lo", "core", "near", "far"),
    )
    where = ("z_hi", "z_lo", "core", "near", "far")
    return jax.shard_map(
        shards,
        mesh=split,
        in_specs=(P(where, None), P(where, None), P(where), P(where)),
        out_specs=P(where, None),
        check_vma=False,
    )
```

```python
import functools

import jax
import jax.numpy as jnp
from jax import lax
from jax.experimental import pallas as pl
from jax.experimental.pallas import tpu as pltpu
from jax.sharding import Mesh, PartitionSpec as P

SUBKEYS = 4
SOURCES = 4
CODES = SUBKEYS * SOURCES
EPSILON = 1e-06
SHARPNESS = 4.0
LOG2E = 1.4426950408889634
PAD = 8
SWAP = [(0, 1), (1, 0)]
NT = (((1,), (1,)), ((), ()))
VMEM_LIMIT = 48 * 2**20


def owners_here(flips):
    core = lax.axis_index("core")
    spot = lax.axis_index("z_lo") * lax.axis_size("near") + lax.axis_index("near")
    mine = [spot ^ jnp.where(core == 0, a, b) for a, b in zip(*flips)]
    return mine, [spot ^ jnp.where(core == 0, b, a) for a, b in zip(*flips)]


def selections(full_codes, owners, cap):
    rows = full_codes.shape[1]
    count = len(owners)
    lines = max(8, count)
    line = lax.broadcasted_iota(jnp.int32, (lines, rows), 0)
    wanted = jnp.full((lines, rows), -1, jnp.int32)
    for j in range(count):
        wanted = jnp.where(line == j, owners[j], wanted)
    named = wanted == jnp.broadcast_to(full_codes // CODES, (lines, rows))
    before = lax.broadcasted_iota(jnp.int32, (rows, rows), 0)
    after = lax.broadcasted_iota(jnp.int32, (rows, rows), 1)
    earlier = jnp.where(before < after, 1.0, 0.0).astype(jnp.bfloat16)
    rank = jnp.dot(
        jnp.where(named, 1.0, 0.0).astype(jnp.bfloat16),
        earlier,
        preferred_element_type=jnp.float32,
    )
    rank = jnp.where(named, rank, -1.0).astype(jnp.int32)
    slot = lax.broadcasted_iota(jnp.int32, (cap, rows), 0)
    return [
        jnp.where(slot == rank[j : j + 1, :], 1.0, 0.0).astype(jnp.bfloat16)
        for j in range(count)
    ]


def scale_kernel(rows_hbm, owner_hbm, subkey_hbm, source_hbm, out_ref, rows_ref, ids_ref, sems):
    rows, width = rows_ref.shape
    copies = [pltpu.make_async_copy(rows_hbm, rows_ref, sems.at[0])]
    for i, hbm in enumerate((owner_hbm, subkey_hbm, source_hbm)):
        copies.append(pltpu.make_async_copy(hbm, ids_ref.at[i], sems.at[i + 1]))
    for copy in copies:
        copy.start()
    for copy in copies:
        copy.wait()
    values = rows_ref[...].astype(jnp.float32)
    inverse = lax.rsqrt(jnp.mean(values * values, axis=1, keepdims=True) + EPSILON)
    out_ref[:rows, :] = (values * inverse).astype(jnp.bfloat16)
    codes = (ids_ref[0] * SUBKEYS + ids_ref[1]) * SOURCES + ids_ref[2]
    line = lax.broadcasted_iota(jnp.int32, (PAD, width), 0)
    lines = jnp.zeros((PAD, width), jnp.int32)
    for k in range(rows // width):
        lines = jnp.where(line == k, codes[:, k * width : (k + 1) * width], lines)
    out_ref[rows:, :] = lines.astype(jnp.float32).astype(jnp.bfloat16)


def scale(records, owner, subkey, source):
    rows, width = records.shape
    return pl.pallas_call(
        scale_kernel,
        in_specs=[pl.BlockSpec(memory_space=pltpu.HBM)] * 4,
        out_specs=pl.BlockSpec(memory_space=pltpu.VMEM),
        out_shape=jax.ShapeDtypeStruct((rows + PAD, width), jnp.bfloat16),
        scratch_shapes=[
            pltpu.VMEM((rows, width), jnp.bfloat16),
            pltpu.VMEM((3, 1, rows), jnp.int32),
            pltpu.SemaphoreType.DMA((4,)),
        ],
        compiler_params=pltpu.CompilerParams(vmem_limit_bytes=VMEM_LIMIT),
    )(
        *(
            pltpu.with_memory_space_constraint(x, pltpu.HBM)
            for x in (records, *(i.reshape(1, rows) for i in (owner, subkey, source)))
        )
    )


def pack_kernel(flips, cap, *refs):
    blocks, messages = refs[:2], refs[2:]
    count = len(messages)
    owners, _ = owners_here(flips)
    for part in range(2):
        width = blocks[part].shape[1]
        rows = blocks[part].shape[0] - PAD
        scaled = blocks[part][:rows, :]
        lines = blocks[part][rows:, :].astype(jnp.float32)
        full_codes = jnp.concatenate(
            [lines[k : k + 1, :] for k in range(rows // width)], axis=1
        ).astype(jnp.int32)
        codes = jnp.broadcast_to(full_codes % CODES + 1, (8, rows))
        codes = codes.astype(jnp.float32).astype(jnp.bfloat16)
        picks = selections(full_codes, owners, cap)
        for j in range(count):
            picked = jnp.dot(picks[j], scaled, preferred_element_type=jnp.float32)
            messages[j][part, :cap, :] = picked.astype(jnp.bfloat16)
            line = lax.dot_general(codes, picks[j], NT, preferred_element_type=jnp.float32)
            messages[j][part, cap:, :] = jnp.zeros((PAD, width), jnp.bfloat16)
            messages[j][part, cap:, :cap] = line.astype(jnp.bfloat16)


def pack(blocks, flips, cap):
    count = len(flips[0])
    shape = jax.ShapeDtypeStruct((2, cap + PAD, blocks[0].shape[1]), jnp.bfloat16)
    return pl.pallas_call(
        functools.partial(pack_kernel, flips, cap),
        in_specs=[pl.BlockSpec(memory_space=pltpu.VMEM)] * 2,
        out_specs=[pl.BlockSpec(memory_space=pltpu.VMEM)] * count,
        out_shape=[shape] * count,
        compiler_params=pltpu.CompilerParams(vmem_limit_bytes=VMEM_LIMIT),
    )(*blocks)


def place_kernel(flips, cap, owner_ref, out_ref):
    rows = owner_ref.shape[0]
    owner = owner_ref[...]
    lane = lax.broadcasted_iota(jnp.int32, (rows, 128), 1)
    named = owner == lane
    later = lax.broadcasted_iota(jnp.int32, (rows, rows), 0)
    before = lax.broadcasted_iota(jnp.int32, (rows, rows), 1)
    earlier = jnp.where(before < later, 1.0, 0.0).astype(jnp.bfloat16)
    rank = jnp.dot(
        earlier,
        jnp.where(named, 1.0, 0.0).astype(jnp.bfloat16),
        preferred_element_type=jnp.float32,
    )
    rank = jnp.sum(jnp.where(named, rank, 0.0), axis=1, keepdims=True).astype(jnp.int32)
    mine, sibling = owners_here(flips)
    for i, wanted in enumerate(mine + sibling):
        rank = rank + jnp.where(owner == wanted, i * cap, 0)
    out_ref[...] = rank


def place(owner, flips, cap):
    return pl.pallas_call(
        functools.partial(place_kernel, flips, cap),
        in_specs=[pl.BlockSpec(memory_space=pltpu.VMEM)],
        out_specs=pl.BlockSpec(memory_space=pltpu.VMEM),
        out_shape=jax.ShapeDtypeStruct(owner.shape, jnp.int32),
        compiler_params=pltpu.CompilerParams(vmem_limit_bytes=VMEM_LIMIT),
    )(owner)


def code_line(ref, part, cap):
    return ref[part, cap : cap + 8, :cap].astype(jnp.float32)[0:1, :].astype(jnp.int32) - 1


def match_kernel(queries, cap, start, first, last, *refs):
    outs = refs[-queries:] if last else refs[-2:]
    refs = refs[: -queries] if last else refs[:-2]
    held, refs = refs[:queries], refs[queries:]
    sums, keys = (None, refs) if first else (refs[:2], refs[2:])
    width = held[0].shape[2]
    diagonal = lax.broadcasted_iota(jnp.int32, (cap, cap), 0) == lax.broadcasted_iota(
        jnp.int32, (cap, cap), 1
    )
    for j in range(queries):
        query = held[j][:, :cap, :].reshape(2 * cap, width)
        span = slice((start + j) * 2 * cap, (start + j + 1) * 2 * cap)
        columns = []
        for part in range(2):
            line = jnp.broadcast_to(code_line(held[j], part, cap), (cap, cap))
            picked = jnp.where(diagonal, line, 0).astype(jnp.float32)
            columns.append(jnp.sum(picked, axis=1, keepdims=True))
        query_codes = jnp.concatenate(columns, axis=0).astype(jnp.int32)

        def add(key_ref, first, carry):
            total, mass = carry
            pair = key_ref.at[pl.ds(first, 2)]
            key = pair[:, :cap, :].reshape(2 * cap, width)
            key_codes = jnp.concatenate([code_line(pair, k, cap) for k in range(2)], axis=1)
            score = lax.dot_general(query, key, NT, preferred_element_type=jnp.float32)
            differ = query_codes ^ key_codes
            matched = (differ >= 1) & (differ < SOURCES)
            weight = jnp.where(matched, jnp.exp2(score * (SHARPNESS / width * LOG2E)), 0.0)
            mass = mass + jnp.sum(weight, axis=1, keepdims=True)
            return total + jnp.dot(
                weight.astype(jnp.bfloat16), key, preferred_element_type=jnp.float32
            ), mass

        if first:
            carry = jnp.zeros((2 * cap, width), jnp.float32), jnp.zeros((2 * cap, 1), jnp.float32)
        else:
            carry = sums[0][span, :], sums[1][span, :]
        for key_ref in keys:
            pairs = key_ref.shape[0] // 2
            if pairs == 1:
                carry = add(key_ref, 0, carry)
            else:
                carry = lax.fori_loop(
                    0, pairs, lambda i, c, key_ref=key_ref: add(key_ref, 2 * i, c), carry
                )
        total, mass = carry
        if last:
            merged = query.astype(jnp.float32) + total * lax.rsqrt(1.0 + mass)
            outs[j][...] = merged.astype(jnp.bfloat16).reshape(2, cap, width)
        else:
            outs[0][span, :] = total
            outs[1][span, :] = mass


def match(held, keys, cap, sums=None, last=False, start=0):
    count, width = len(held), held[0].shape[2]
    if not last:
        shapes = [
            jax.ShapeDtypeStruct((count * 2 * cap, width), jnp.float32),
            jax.ShapeDtypeStruct((count * 2 * cap, 1), jnp.float32),
        ]
    else:
        shapes = [jax.ShapeDtypeStruct((2, cap, width), jnp.bfloat16)] * count
    operands = (*held, *(sums or ()), *keys)
    return pl.pallas_call(
        functools.partial(match_kernel, count, cap, start, sums is None, last),
        in_specs=[pl.BlockSpec(memory_space=pltpu.VMEM)] * len(operands),
        out_specs=[pl.BlockSpec(memory_space=pltpu.VMEM)] * len(shapes),
        out_shape=shapes,
        compiler_params=pltpu.CompilerParams(vmem_limit_bytes=VMEM_LIMIT),
    )(*operands)


def unpack_kernel(count, cap, place_ref, *refs):
    mine, sibling, out_ref = refs[:count], refs[count : 2 * count], refs[-1]
    rows = out_ref.shape[0]
    slot = lax.broadcasted_iota(jnp.int32, (rows, 2 * count * cap), 1)
    picks = jnp.where(slot == place_ref[...], 1.0, 0.0).astype(jnp.bfloat16)
    blocks = [m[0] for m in mine] + [m[1] for m in sibling]
    out_ref[...] = jnp.dot(
        picks, jnp.concatenate(blocks, axis=0), preferred_element_type=jnp.float32
    ).astype(jnp.bfloat16)


def unpack(places, mine, sibling, cap):
    count, width = len(mine), mine[0].shape[2]
    return pl.pallas_call(
        functools.partial(unpack_kernel, count, cap),
        in_specs=[pl.BlockSpec(memory_space=pltpu.VMEM)] * (2 * count + 1),
        out_specs=pl.BlockSpec(memory_space=pltpu.VMEM),
        out_shape=jax.ShapeDtypeStruct((places.shape[0], width), jnp.bfloat16),
        compiler_params=pltpu.CompilerParams(vmem_limit_bytes=VMEM_LIMIT),
    )(places, *mine, *sibling)


def shards(records, owner, subkey, source):
    row_count = records.shape[0]
    chips = lax.axis_size("z_lo") * lax.axis_size("near")
    near, rest = lax.axis_size("near"), lax.axis_size("far")
    cap = 2 * row_count // chips
    by_hops = sorted(range(chips), key=lambda d: (-(d // near), -d.bit_count()))
    flips = [[d for d in by_hops if d.bit_count() % 2 == odd] for odd in (1, 0)]
    def to_core(x):
        return lax.ppermute(x, "core", SWAP)

    def to_half(x):
        return lax.ppermute(x, "z_hi", SWAP)

    def to_chip(x, j, back=False):
        def number(c, s):
            return (s // near * 2 + c) * near + s % near

        pairs = []
        for s in range(chips):
            stays = flips[1][j] == 0
            pairs.append((number(0, s), number(1 if stays else 0, s ^ flips[0][j])))
            pairs.append((number(1, s), number(0 if stays else 1, s ^ flips[1][j])))
        if back:
            pairs = [(target, origin) for origin, target in pairs]
        return lax.ppermute(x, ("z_lo", "core", "near"), pairs)

    def gathered(messages):
        if rest > 1:
            return [lax.all_gather(m, "far", axis=0, tiled=True) for m in messages]
        return messages

    block = scale(records, owner, subkey, source)
    far_block = to_half(block)
    places = place(owner, flips, cap)
    held = [to_chip(m, j) for j, m in enumerate(pack((block, to_core(block)), flips, cap))]
    far_block, places, held = lax.optimization_barrier((far_block, places, held))
    near_keys = gathered(held)
    near_keys = near_keys + [to_core(m) for m in near_keys]
    far_messages = pack((far_block, to_core(far_block)), flips, cap)
    near_keys, _ = lax.optimization_barrier((near_keys, far_messages[0]))
    far_keys = gathered([to_chip(m, j) for j, m in enumerate(far_messages)])
    sums = match(held, near_keys, cap)
    sums, far_keys = lax.optimization_barrier((sums, far_keys))
    swapped = [to_core(m) for m in far_keys]
    sums = match(held, far_keys, cap, sums)
    merged = match(held, swapped, cap, sums, last=True)
    returned = [to_chip(m, j, back=True) for j, m in enumerate(merged)]
    return unpack(places, returned, [to_core(m) for m in returned], cap)


def solution(mesh):
    own, help_ = mesh.shape["own"], mesh.shape["help"]
    near = 4
    split = Mesh(
        mesh.devices.reshape(2, own // 4, 2, near, help_ // near),
        ("z_hi", "z_lo", "core", "near", "far"),
    )
    where = ("z_hi", "z_lo", "core", "near", "far")
    return jax.shard_map(
        shards,
        mesh=split,
        in_specs=(P(where, None), P(where, None), P(where), P(where)),
        out_specs=P(where, None),
        check_vma=False,
    )
```

```python
import functools

import jax
import jax.numpy as jnp
from jax import lax
from jax.experimental import pallas as pl
from jax.experimental.pallas import tpu as pltpu
from jax.sharding import Mesh, PartitionSpec as P

SUBKEYS = 4
SOURCES = 4
CODES = SUBKEYS * SOURCES
EPSILON = 1e-06
SHARPNESS = 4.0
LOG2E = 1.4426950408889634
PAD = 8
SWAP = [(0, 1), (1, 0)]
NT = (((1,), (1,)), ((), ()))
VMEM_LIMIT = 48 * 2**20


def owners_here(flips):
    core = lax.axis_index("core")
    spot = lax.axis_index("z_lo") * lax.axis_size("near") + lax.axis_index("near")
    mine = [spot ^ jnp.where(core == 0, a, b) for a, b in zip(*flips)]
    return mine, [spot ^ jnp.where(core == 0, b, a) for a, b in zip(*flips)]


def selections(full_codes, owners, cap):
    rows = full_codes.shape[1]
    count = len(owners)
    lines = max(8, count)
    line = lax.broadcasted_iota(jnp.int32, (lines, rows), 0)
    wanted = jnp.full((lines, rows), -1, jnp.int32)
    for j in range(count):
        wanted = jnp.where(line == j, owners[j], wanted)
    named = wanted == jnp.broadcast_to(full_codes // CODES, (lines, rows))
    before = lax.broadcasted_iota(jnp.int32, (rows, rows), 0)
    after = lax.broadcasted_iota(jnp.int32, (rows, rows), 1)
    earlier = jnp.where(before < after, 1.0, 0.0).astype(jnp.bfloat16)
    rank = jnp.dot(
        jnp.where(named, 1.0, 0.0).astype(jnp.bfloat16),
        earlier,
        preferred_element_type=jnp.float32,
    )
    rank = jnp.where(named, rank, -1.0).astype(jnp.int32)
    slot = lax.broadcasted_iota(jnp.int32, (cap, rows), 0)
    return [
        jnp.where(slot == rank[j : j + 1, :], 1.0, 0.0).astype(jnp.bfloat16)
        for j in range(count)
    ]


def scale_kernel(rows_hbm, owner_hbm, subkey_hbm, source_hbm, out_ref, rows_ref, ids_ref, sems):
    rows, width = rows_ref.shape
    copies = [pltpu.make_async_copy(rows_hbm, rows_ref, sems.at[0])]
    for i, hbm in enumerate((owner_hbm, subkey_hbm, source_hbm)):
        copies.append(pltpu.make_async_copy(hbm, ids_ref.at[i], sems.at[i + 1]))
    for copy in copies:
        copy.start()
    for copy in copies:
        copy.wait()
    values = rows_ref[...].astype(jnp.float32)
    inverse = lax.rsqrt(jnp.mean(values * values, axis=1, keepdims=True) + EPSILON)
    out_ref[:rows, :] = (values * inverse).astype(jnp.bfloat16)
    codes = (ids_ref[0] * SUBKEYS + ids_ref[1]) * SOURCES + ids_ref[2]
    line = lax.broadcasted_iota(jnp.int32, (PAD, width), 0)
    lines = jnp.zeros((PAD, width), jnp.int32)
    for k in range(rows // width):
        lines = jnp.where(line == k, codes[:, k * width : (k + 1) * width], lines)
    out_ref[rows:, :] = lines.astype(jnp.float32).astype(jnp.bfloat16)


def scale(records, owner, subkey, source):
    rows, width = records.shape
    return pl.pallas_call(
        scale_kernel,
        in_specs=[pl.BlockSpec(memory_space=pltpu.HBM)] * 4,
        out_specs=pl.BlockSpec(memory_space=pltpu.VMEM),
        out_shape=jax.ShapeDtypeStruct((rows + PAD, width), jnp.bfloat16),
        scratch_shapes=[
            pltpu.VMEM((rows, width), jnp.bfloat16),
            pltpu.VMEM((3, 1, rows), jnp.int32),
            pltpu.SemaphoreType.DMA((4,)),
        ],
        compiler_params=pltpu.CompilerParams(vmem_limit_bytes=VMEM_LIMIT),
    )(
        *(
            pltpu.with_memory_space_constraint(x, pltpu.HBM)
            for x in (records, *(i.reshape(1, rows) for i in (owner, subkey, source)))
        )
    )


def pack_kernel(flips, cap, *refs):
    blocks, messages = refs[:2], refs[2:]
    count = len(messages)
    owners, _ = owners_here(flips)
    for part in range(2):
        width = blocks[part].shape[1]
        rows = blocks[part].shape[0] - PAD
        scaled = blocks[part][:rows, :]
        lines = blocks[part][rows:, :].astype(jnp.float32)
        full_codes = jnp.concatenate(
            [lines[k : k + 1, :] for k in range(rows // width)], axis=1
        ).astype(jnp.int32)
        codes = jnp.broadcast_to(full_codes % CODES + 1, (8, rows))
        codes = codes.astype(jnp.float32).astype(jnp.bfloat16)
        picks = selections(full_codes, owners, cap)
        for j in range(count):
            picked = jnp.dot(picks[j], scaled, preferred_element_type=jnp.float32)
            messages[j][part, :cap, :] = picked.astype(jnp.bfloat16)
            line = lax.dot_general(codes, picks[j], NT, preferred_element_type=jnp.float32)
            messages[j][part, cap:, :] = jnp.zeros((PAD, width), jnp.bfloat16)
            messages[j][part, cap:, :cap] = line.astype(jnp.bfloat16)


def pack(blocks, flips, cap):
    count = len(flips[0])
    shape = jax.ShapeDtypeStruct((2, cap + PAD, blocks[0].shape[1]), jnp.bfloat16)
    return pl.pallas_call(
        functools.partial(pack_kernel, flips, cap),
        in_specs=[pl.BlockSpec(memory_space=pltpu.VMEM)] * 2,
        out_specs=[pl.BlockSpec(memory_space=pltpu.VMEM)] * count,
        out_shape=[shape] * count,
        compiler_params=pltpu.CompilerParams(vmem_limit_bytes=VMEM_LIMIT),
    )(*blocks)


def place_kernel(flips, cap, owner_ref, out_ref):
    rows = owner_ref.shape[0]
    owner = owner_ref[...]
    lane = lax.broadcasted_iota(jnp.int32, (rows, 128), 1)
    named = owner == lane
    later = lax.broadcasted_iota(jnp.int32, (rows, rows), 0)
    before = lax.broadcasted_iota(jnp.int32, (rows, rows), 1)
    earlier = jnp.where(before < later, 1.0, 0.0).astype(jnp.bfloat16)
    rank = jnp.dot(
        earlier,
        jnp.where(named, 1.0, 0.0).astype(jnp.bfloat16),
        preferred_element_type=jnp.float32,
    )
    rank = jnp.sum(jnp.where(named, rank, 0.0), axis=1, keepdims=True).astype(jnp.int32)
    mine, sibling = owners_here(flips)
    for i, wanted in enumerate(mine + sibling):
        rank = rank + jnp.where(owner == wanted, i * cap, 0)
    out_ref[...] = rank


def place(owner, flips, cap):
    return pl.pallas_call(
        functools.partial(place_kernel, flips, cap),
        in_specs=[pl.BlockSpec(memory_space=pltpu.VMEM)],
        out_specs=pl.BlockSpec(memory_space=pltpu.VMEM),
        out_shape=jax.ShapeDtypeStruct(owner.shape, jnp.int32),
        compiler_params=pltpu.CompilerParams(vmem_limit_bytes=VMEM_LIMIT),
    )(owner)


def code_line(ref, part, cap):
    return ref[part, cap : cap + 8, :cap].astype(jnp.float32)[0:1, :].astype(jnp.int32) - 1


def match_kernel(queries, cap, start, first, last, *refs):
    outs = refs[-queries:] if last else refs[-2:]
    refs = refs[: -queries] if last else refs[:-2]
    held, refs = refs[:queries], refs[queries:]
    sums, keys = (None, refs) if first else (refs[:2], refs[2:])
    width = held[0].shape[2]
    diagonal = lax.broadcasted_iota(jnp.int32, (cap, cap), 0) == lax.broadcasted_iota(
        jnp.int32, (cap, cap), 1
    )
    for j in range(queries):
        query = held[j][:, :cap, :].reshape(2 * cap, width)
        span = slice((start + j) * 2 * cap, (start + j + 1) * 2 * cap)
        columns = []
        for part in range(2):
            line = jnp.broadcast_to(code_line(held[j], part, cap), (cap, cap))
            picked = jnp.where(diagonal, line, 0).astype(jnp.float32)
            columns.append(jnp.sum(picked, axis=1, keepdims=True))
        query_codes = jnp.concatenate(columns, axis=0).astype(jnp.int32)

        def add(key_ref, first, carry):
            total, mass = carry
            pair = key_ref.at[pl.ds(first, 2)]
            key = pair[:, :cap, :].reshape(2 * cap, width)
            key_codes = jnp.concatenate([code_line(pair, k, cap) for k in range(2)], axis=1)
            score = lax.dot_general(query, key, NT, preferred_element_type=jnp.float32)
            differ = query_codes ^ key_codes
            matched = (differ >= 1) & (differ < SOURCES)
            weight = jnp.where(matched, jnp.exp2(score * (SHARPNESS / width * LOG2E)), 0.0)
            mass = mass + jnp.sum(weight, axis=1, keepdims=True)
            return total + jnp.dot(
                weight.astype(jnp.bfloat16), key, preferred_element_type=jnp.float32
            ), mass

        if first:
            carry = jnp.zeros((2 * cap, width), jnp.float32), jnp.zeros((2 * cap, 1), jnp.float32)
        else:
            carry = sums[0][span, :], sums[1][span, :]
        for key_ref in keys:
            pairs = key_ref.shape[0] // 2
            if pairs == 1:
                carry = add(key_ref, 0, carry)
            else:
                carry = lax.fori_loop(
                    0, pairs, lambda i, c, key_ref=key_ref: add(key_ref, 2 * i, c), carry
                )
        total, mass = carry
        if last:
            merged = query.astype(jnp.float32) + total * lax.rsqrt(1.0 + mass)
            outs[j][...] = merged.astype(jnp.bfloat16).reshape(2, cap, width)
        else:
            outs[0][span, :] = total
            outs[1][span, :] = mass


def match(held, keys, cap, sums=None, last=False, start=0):
    count, width = len(held), held[0].shape[2]
    if not last:
        shapes = [
            jax.ShapeDtypeStruct((count * 2 * cap, width), jnp.float32),
            jax.ShapeDtypeStruct((count * 2 * cap, 1), jnp.float32),
        ]
    else:
        shapes = [jax.ShapeDtypeStruct((2, cap, width), jnp.bfloat16)] * count
    operands = (*held, *(sums or ()), *keys)
    return pl.pallas_call(
        functools.partial(match_kernel, count, cap, start, sums is None, last),
        in_specs=[pl.BlockSpec(memory_space=pltpu.VMEM)] * len(operands),
        out_specs=[pl.BlockSpec(memory_space=pltpu.VMEM)] * len(shapes),
        out_shape=shapes,
        compiler_params=pltpu.CompilerParams(vmem_limit_bytes=VMEM_LIMIT),
    )(*operands)


def unpack_kernel(spots, cap, more, place_ref, *refs):
    blocks, out_ref = refs[: len(spots)], refs[-1]
    rows = out_ref.shape[0]
    slot = lax.broadcasted_iota(jnp.int32, (rows, cap), 1)
    picks = [jnp.where(slot + i * cap == place_ref[...], 1.0, 0.0).astype(jnp.bfloat16) for i, _ in spots]
    found = jnp.dot(
        jnp.concatenate(picks, axis=1),
        jnp.concatenate([ref[part] for ref, (_, part) in zip(blocks, spots)], axis=0),
        preferred_element_type=jnp.float32,
    ).astype(jnp.bfloat16)
    out_ref[...] = refs[len(spots)][...] + found if more else found


def unpack(places, blocks, spots, cap, earlier=None):
    operands = (places, *blocks, *(() if earlier is None else (earlier,)))
    return pl.pallas_call(
        functools.partial(unpack_kernel, spots, cap, earlier is not None),
        in_specs=[pl.BlockSpec(memory_space=pltpu.VMEM)] * len(operands),
        out_specs=pl.BlockSpec(memory_space=pltpu.VMEM),
        out_shape=jax.ShapeDtypeStruct((places.shape[0], blocks[0].shape[2]), jnp.bfloat16),
        compiler_params=pltpu.CompilerParams(vmem_limit_bytes=VMEM_LIMIT),
    )(*operands)


def shards(records, owner, subkey, source):
    row_count = records.shape[0]
    chips = lax.axis_size("z_lo") * lax.axis_size("near")
    near, rest = lax.axis_size("near"), lax.axis_size("far")
    cap = 2 * row_count // chips
    by_hops = sorted(range(chips), key=lambda d: (-(d // near), -d.bit_count()))
    flips = [[d for d in by_hops if d.bit_count() % 2 == odd] for odd in (1, 0)]
    def to_core(x):
        return lax.ppermute(x, "core", SWAP)

    def to_half(x):
        return lax.ppermute(x, "z_hi", SWAP)

    def to_chip(x, j, back=False):
        def number(c, s):
            return (s // near * 2 + c) * near + s % near

        pairs = []
        for s in range(chips):
            stays = flips[1][j] == 0
            pairs.append((number(0, s), number(1 if stays else 0, s ^ flips[0][j])))
            pairs.append((number(1, s), number(0 if stays else 1, s ^ flips[1][j])))
        if back:
            pairs = [(target, origin) for origin, target in pairs]
        return lax.ppermute(x, ("z_lo", "core", "near"), pairs)

    def gathered(messages):
        if rest > 1:
            return [lax.all_gather(m, "far", axis=0, tiled=True) for m in messages]
        return messages

    block = scale(records, owner, subkey, source)
    far_block = to_half(block)
    places = place(owner, flips, cap)
    held = [to_chip(m, j) for j, m in enumerate(pack((block, to_core(block)), flips, cap))]
    far_block, places, held = lax.optimization_barrier((far_block, places, held))
    near_keys = gathered(held)
    near_keys = near_keys + [to_core(m) for m in near_keys]
    far_messages = pack((far_block, to_core(far_block)), flips, cap)
    near_keys, _ = lax.optimization_barrier((near_keys, far_messages[0]))
    far_keys = gathered([to_chip(m, j) for j, m in enumerate(far_messages)])
    sums = match(held, near_keys, cap)
    sums, far_keys = lax.optimization_barrier((sums, far_keys))
    swapped = [to_core(m) for m in far_keys]
    sums = match(held, far_keys, cap, sums)
    half = len(held) // 2
    merged = match(held[:half], swapped, cap, sums, True)
    sums, merged = lax.optimization_barrier((sums, merged))
    merged = merged + match(held[half:], swapped, cap, sums, True, half)
    returned = [to_chip(m, j, back=True) for j, m in enumerate(merged)]
    count = len(returned)
    swapped = [to_core(m) for m in returned]
    early = unpack(places, returned, [(j, 0) for j in range(count)], cap)
    return unpack(places, swapped, [(count + j, 1) for j in range(count)], cap, early)


def solution(mesh):
    own, help_ = mesh.shape["own"], mesh.shape["help"]
    near = 4
    split = Mesh(
        mesh.devices.reshape(2, own // 4, 2, near, help_ // near),
        ("z_hi", "z_lo", "core", "near", "far"),
    )
    where = ("z_hi", "z_lo", "core", "near", "far")
    return jax.shard_map(
        shards,
        mesh=split,
        in_specs=(P(where, None), P(where, None), P(where), P(where)),
        out_specs=P(where, None),
        check_vma=False,
    )
```

```python
import functools

import jax
import jax.numpy as jnp
from jax import lax
from jax.experimental import pallas as pl
from jax.experimental.pallas import tpu as pltpu
from jax.sharding import Mesh, PartitionSpec as P

SUBKEYS = 4
SOURCES = 4
CODES = SUBKEYS * SOURCES
EPSILON = 1e-06
SHARPNESS = 4.0
LOG2E = 1.4426950408889634
PAD = 8
SWAP = [(0, 1), (1, 0)]
NT = (((1,), (1,)), ((), ()))
VMEM_LIMIT = 48 * 2**20


def owners_here(flips):
    core = lax.axis_index("core")
    spot = lax.axis_index("z_lo") * lax.axis_size("near") + lax.axis_index("near")
    mine = [spot ^ jnp.where(core == 0, a, b) for a, b in zip(*flips)]
    return mine, [spot ^ jnp.where(core == 0, b, a) for a, b in zip(*flips)]


def selections(full_codes, owners, cap):
    rows = full_codes.shape[1]
    count = len(owners)
    lines = max(8, count)
    line = lax.broadcasted_iota(jnp.int32, (lines, rows), 0)
    wanted = jnp.full((lines, rows), -1, jnp.int32)
    for j in range(count):
        wanted = jnp.where(line == j, owners[j], wanted)
    named = wanted == jnp.broadcast_to(full_codes // CODES, (lines, rows))
    before = lax.broadcasted_iota(jnp.int32, (rows, rows), 0)
    after = lax.broadcasted_iota(jnp.int32, (rows, rows), 1)
    earlier = jnp.where(before < after, 1.0, 0.0).astype(jnp.bfloat16)
    rank = jnp.dot(
        jnp.where(named, 1.0, 0.0).astype(jnp.bfloat16),
        earlier,
        preferred_element_type=jnp.float32,
    )
    rank = jnp.where(named, rank, -1.0).astype(jnp.int32)
    slot = lax.broadcasted_iota(jnp.int32, (cap, rows), 0)
    return [
        jnp.where(slot == rank[j : j + 1, :], 1.0, 0.0).astype(jnp.bfloat16)
        for j in range(count)
    ]


def scale_kernel(rows_hbm, owner_hbm, subkey_hbm, source_hbm, out_ref, rows_ref, ids_ref, sems):
    rows, width = rows_ref.shape
    copies = [pltpu.make_async_copy(rows_hbm, rows_ref, sems.at[0])]
    for i, hbm in enumerate((owner_hbm, subkey_hbm, source_hbm)):
        copies.append(pltpu.make_async_copy(hbm, ids_ref.at[i], sems.at[i + 1]))
    for copy in copies:
        copy.start()
    for copy in copies:
        copy.wait()
    values = rows_ref[...].astype(jnp.float32)
    inverse = lax.rsqrt(jnp.mean(values * values, axis=1, keepdims=True) + EPSILON)
    out_ref[:rows, :] = (values * inverse).astype(jnp.bfloat16)
    codes = (ids_ref[0] * SUBKEYS + ids_ref[1]) * SOURCES + ids_ref[2]
    line = lax.broadcasted_iota(jnp.int32, (PAD, width), 0)
    lines = jnp.zeros((PAD, width), jnp.int32)
    for k in range(rows // width):
        lines = jnp.where(line == k, codes[:, k * width : (k + 1) * width], lines)
    out_ref[rows:, :] = lines.astype(jnp.float32).astype(jnp.bfloat16)


def scale(records, owner, subkey, source):
    rows, width = records.shape
    return pl.pallas_call(
        scale_kernel,
        in_specs=[pl.BlockSpec(memory_space=pltpu.HBM)] * 4,
        out_specs=pl.BlockSpec(memory_space=pltpu.VMEM),
        out_shape=jax.ShapeDtypeStruct((rows + PAD, width), jnp.bfloat16),
        scratch_shapes=[
            pltpu.VMEM((rows, width), jnp.bfloat16),
            pltpu.VMEM((3, 1, rows), jnp.int32),
            pltpu.SemaphoreType.DMA((4,)),
        ],
        compiler_params=pltpu.CompilerParams(vmem_limit_bytes=VMEM_LIMIT),
    )(
        *(
            pltpu.with_memory_space_constraint(x, pltpu.HBM)
            for x in (records, *(i.reshape(1, rows) for i in (owner, subkey, source)))
        )
    )


def pack_kernel(flips, cap, *refs):
    blocks, messages = refs[:2], refs[2:]
    count = len(messages)
    owners, _ = owners_here(flips)
    for part in range(2):
        width = blocks[part].shape[1]
        rows = blocks[part].shape[0] - PAD
        scaled = blocks[part][:rows, :]
        lines = blocks[part][rows:, :].astype(jnp.float32)
        full_codes = jnp.concatenate(
            [lines[k : k + 1, :] for k in range(rows // width)], axis=1
        ).astype(jnp.int32)
        codes = jnp.broadcast_to(full_codes % CODES + 1, (8, rows))
        codes = codes.astype(jnp.float32).astype(jnp.bfloat16)
        picks = selections(full_codes, owners, cap)
        for j in range(count):
            picked = jnp.dot(picks[j], scaled, preferred_element_type=jnp.float32)
            messages[j][part, :cap, :] = picked.astype(jnp.bfloat16)
            line = lax.dot_general(codes, picks[j], NT, preferred_element_type=jnp.float32)
            messages[j][part, cap:, :] = jnp.zeros((PAD, width), jnp.bfloat16)
            messages[j][part, cap:, :cap] = line.astype(jnp.bfloat16)


def pack(blocks, flips, cap):
    count = len(flips[0])
    shape = jax.ShapeDtypeStruct((2, cap + PAD, blocks[0].shape[1]), jnp.bfloat16)
    return pl.pallas_call(
        functools.partial(pack_kernel, flips, cap),
        in_specs=[pl.BlockSpec(memory_space=pltpu.VMEM)] * 2,
        out_specs=[pl.BlockSpec(memory_space=pltpu.VMEM)] * count,
        out_shape=[shape] * count,
        compiler_params=pltpu.CompilerParams(vmem_limit_bytes=VMEM_LIMIT),
    )(*blocks)


def place_kernel(flips, cap, owner_ref, out_ref):
    rows = owner_ref.shape[0]
    owner = owner_ref[...]
    lane = lax.broadcasted_iota(jnp.int32, (rows, 128), 1)
    named = owner == lane
    later = lax.broadcasted_iota(jnp.int32, (rows, rows), 0)
    before = lax.broadcasted_iota(jnp.int32, (rows, rows), 1)
    earlier = jnp.where(before < later, 1.0, 0.0).astype(jnp.bfloat16)
    rank = jnp.dot(
        earlier,
        jnp.where(named, 1.0, 0.0).astype(jnp.bfloat16),
        preferred_element_type=jnp.float32,
    )
    rank = jnp.sum(jnp.where(named, rank, 0.0), axis=1, keepdims=True).astype(jnp.int32)
    mine, sibling = owners_here(flips)
    for i, wanted in enumerate(mine + sibling):
        rank = rank + jnp.where(owner == wanted, i * cap, 0)
    out_ref[...] = rank


def place(owner, flips, cap):
    return pl.pallas_call(
        functools.partial(place_kernel, flips, cap),
        in_specs=[pl.BlockSpec(memory_space=pltpu.VMEM)],
        out_specs=pl.BlockSpec(memory_space=pltpu.VMEM),
        out_shape=jax.ShapeDtypeStruct(owner.shape, jnp.int32),
        compiler_params=pltpu.CompilerParams(vmem_limit_bytes=VMEM_LIMIT),
    )(owner)


def code_line(ref, part, cap):
    return ref[part, cap : cap + 8, :cap].astype(jnp.float32)[0:1, :].astype(jnp.int32) - 1


def match_kernel(queries, cap, start, first, last, *refs):
    outs = refs[-queries:] if last else refs[-2:]
    refs = refs[: -queries] if last else refs[:-2]
    held, refs = refs[:queries], refs[queries:]
    sums, keys = (None, refs) if first else (refs[:2], refs[2:])
    width = held[0].shape[2]
    diagonal = lax.broadcasted_iota(jnp.int32, (cap, cap), 0) == lax.broadcasted_iota(
        jnp.int32, (cap, cap), 1
    )
    for j in range(queries):
        query = held[j][:, :cap, :].reshape(2 * cap, width)
        span = slice((start + j) * 2 * cap, (start + j + 1) * 2 * cap)
        columns = []
        for part in range(2):
            line = jnp.broadcast_to(code_line(held[j], part, cap), (cap, cap))
            picked = jnp.where(diagonal, line, 0).astype(jnp.float32)
            columns.append(jnp.sum(picked, axis=1, keepdims=True))
        query_codes = jnp.concatenate(columns, axis=0).astype(jnp.int32)

        def add(key_ref, first, carry):
            total, mass = carry
            pair = key_ref.at[pl.ds(first, 2)]
            key = pair[:, :cap, :].reshape(2 * cap, width)
            key_codes = jnp.concatenate([code_line(pair, k, cap) for k in range(2)], axis=1)
            score = lax.dot_general(query, key, NT, preferred_element_type=jnp.float32)
            differ = query_codes ^ key_codes
            matched = (differ >= 1) & (differ < SOURCES)
            weight = jnp.where(matched, jnp.exp2(score * (SHARPNESS / width * LOG2E)), 0.0)
            mass = mass + jnp.sum(weight, axis=1, keepdims=True)
            return total + jnp.dot(
                weight.astype(jnp.bfloat16), key, preferred_element_type=jnp.float32
            ), mass

        if first:
            carry = jnp.zeros((2 * cap, width), jnp.float32), jnp.zeros((2 * cap, 1), jnp.float32)
        else:
            carry = sums[0][span, :], sums[1][span, :]
        for key_ref in keys:
            pairs = key_ref.shape[0] // 2
            if pairs == 1:
                carry = add(key_ref, 0, carry)
            else:
                carry = lax.fori_loop(
                    0, pairs, lambda i, c, key_ref=key_ref: add(key_ref, 2 * i, c), carry
                )
        total, mass = carry
        if last:
            merged = query.astype(jnp.float32) + total * lax.rsqrt(1.0 + mass)
            outs[j][...] = merged.astype(jnp.bfloat16).reshape(2, cap, width)
        else:
            outs[0][span, :] = total
            outs[1][span, :] = mass


def match(held, keys, cap, sums=None, last=False, start=0):
    count, width = len(held), held[0].shape[2]
    if not last:
        shapes = [
            jax.ShapeDtypeStruct((count * 2 * cap, width), jnp.float32),
            jax.ShapeDtypeStruct((count * 2 * cap, 1), jnp.float32),
        ]
    else:
        shapes = [jax.ShapeDtypeStruct((2, cap, width), jnp.bfloat16)] * count
    operands = (*held, *(sums or ()), *keys)
    return pl.pallas_call(
        functools.partial(match_kernel, count, cap, start, sums is None, last),
        in_specs=[pl.BlockSpec(memory_space=pltpu.VMEM)] * len(operands),
        out_specs=[pl.BlockSpec(memory_space=pltpu.VMEM)] * len(shapes),
        out_shape=shapes,
        compiler_params=pltpu.CompilerParams(vmem_limit_bytes=VMEM_LIMIT),
    )(*operands)


def unpack_kernel(spots, cap, more, place_ref, *refs):
    blocks, out_ref = refs[: len(spots)], refs[-1]
    rows = out_ref.shape[0]
    slot = lax.broadcasted_iota(jnp.int32, (rows, cap), 1)
    picks = [jnp.where(slot + i * cap == place_ref[...], 1.0, 0.0).astype(jnp.bfloat16) for i, _ in spots]
    found = jnp.dot(
        jnp.concatenate(picks, axis=1),
        jnp.concatenate([ref[part] for ref, (_, part) in zip(blocks, spots)], axis=0),
        preferred_element_type=jnp.float32,
    ).astype(jnp.bfloat16)
    out_ref[...] = refs[len(spots)][...] + found if more else found


def unpack(places, blocks, spots, cap, earlier=None):
    operands = (places, *blocks, *(() if earlier is None else (earlier,)))
    return pl.pallas_call(
        functools.partial(unpack_kernel, spots, cap, earlier is not None),
        in_specs=[pl.BlockSpec(memory_space=pltpu.VMEM)] * len(operands),
        out_specs=pl.BlockSpec(memory_space=pltpu.VMEM),
        out_shape=jax.ShapeDtypeStruct((places.shape[0], blocks[0].shape[2]), jnp.bfloat16),
        compiler_params=pltpu.CompilerParams(vmem_limit_bytes=VMEM_LIMIT),
    )(*operands)


def shards(records, owner, subkey, source):
    row_count = records.shape[0]
    chips = lax.axis_size("z_lo") * lax.axis_size("near")
    near, rest = lax.axis_size("near"), lax.axis_size("far")
    cap = 2 * row_count // chips
    by_hops = sorted(range(chips), key=lambda d: (-(d // near), -d.bit_count()))
    flips = [[d for d in by_hops if d.bit_count() % 2 == odd] for odd in (1, 0)]
    def to_core(x):
        return lax.ppermute(x, "core", SWAP)

    def to_half(x):
        return lax.ppermute(x, "z_hi", SWAP)

    def to_chip(x, j, back=False):
        def number(c, s):
            return (s // near * 2 + c) * near + s % near

        pairs = []
        for s in range(chips):
            stays = flips[1][j] == 0
            pairs.append((number(0, s), number(1 if stays else 0, s ^ flips[0][j])))
            pairs.append((number(1, s), number(0 if stays else 1, s ^ flips[1][j])))
        if back:
            pairs = [(target, origin) for origin, target in pairs]
        return lax.ppermute(x, ("z_lo", "core", "near"), pairs)

    def gathered(messages):
        if rest > 1:
            return [lax.all_gather(m, "far", axis=0, tiled=True) for m in messages]
        return messages

    block = scale(records, owner, subkey, source)
    far_block = to_half(block)
    places = place(owner, flips, cap)
    half = chips // 4
    pair = (block, to_core(block))
    messages = pack(pair, [f[:half] for f in flips], cap)
    pair, messages = lax.optimization_barrier((pair, messages))
    messages = messages + pack(pair, [f[half:] for f in flips], cap)
    held = [to_chip(m, j) for j, m in enumerate(messages)]
    far_block, places, held = lax.optimization_barrier((far_block, places, held))
    near_keys = gathered(held)
    near_keys = near_keys + [to_core(m) for m in near_keys]
    far_messages = pack((far_block, to_core(far_block)), flips, cap)
    near_keys, _ = lax.optimization_barrier((near_keys, far_messages[0]))
    far_keys = gathered([to_chip(m, j) for j, m in enumerate(far_messages)])
    sums = match(held, near_keys, cap)
    sums, far_keys = lax.optimization_barrier((sums, far_keys))
    swapped = [to_core(m) for m in far_keys]
    sums = match(held, far_keys, cap, sums)
    half = len(held) // 2
    merged = match(held[:half], swapped, cap, sums, True)
    sums, merged = lax.optimization_barrier((sums, merged))
    merged = merged + match(held[half:], swapped, cap, sums, True, half)
    returned = [to_chip(m, j, back=True) for j, m in enumerate(merged)]
    count = len(returned)
    swapped = [to_core(m) for m in returned]
    early = unpack(places, returned, [(j, 0) for j in range(count)], cap)
    return unpack(places, swapped, [(count + j, 1) for j in range(count)], cap, early)


def solution(mesh):
    own, help_ = mesh.shape["own"], mesh.shape["help"]
    near = 4
    split = Mesh(
        mesh.devices.reshape(2, own // 4, 2, near, help_ // near),
        ("z_hi", "z_lo", "core", "near", "far"),
    )
    where = ("z_hi", "z_lo", "core", "near", "far")
    return jax.shard_map(
        shards,
        mesh=split,
        in_specs=(P(where, None), P(where, None), P(where), P(where)),
        out_specs=P(where, None),
        check_vma=False,
    )
```
